32 devices in a mesh: dp: 8 (over z, x), tensor: 4 (over y, core).
Axes of the slice: x: 2, y: 2, z: 4, core: 2. Of those that a mesh axis runs over, the one named last changes fastest.
Arguments:
- tokens: bfloat16 [6144, 2304], P(('dp', 'tensor')), may hold values from -6 to 6
- segment_ids: int32 [6144], P('dp'), may hold values from 0 to 11, as said below
- attention_norm: bfloat16 [2304], P('dp'), may hold values from 0.5 to 1.5
- query_weight: bfloat16 [2304, 2048], P('dp', 'tensor'), may hold values from -0.125 to 0.125
- key_matrix: bfloat16 [2304, 1024], P('dp', 'tensor'), may hold values from -0.125 to 0.125
- value_matrix: bfloat16 [2304, 1024], P('dp', 'tensor'), may hold values from -0.125 to 0.125
- output_weight: bfloat16 [2048, 2304], P('tensor', 'dp'), may hold values from -0.25 to 0.25
- attention_post_norm: bfloat16 [2304], P('dp'), may hold values from 0.5 to 1.5
- feedforward_norm: bfloat16 [2304], P('dp'), may hold values from 0.5 to 1.5
- gate_weight: bfloat16 [2304, 9216], P('dp', 'tensor'), may hold values from -0.125 to 0.125
- up_weight: bfloat16 [2304, 9216], P('dp', 'tensor'), may hold values from -0.125 to 0.125
- down_weight: bfloat16 [9216, 2304], P('tensor', 'dp'), may hold values from -0.0625 to 0.0625
- feedforward_post_norm: bfloat16 [2304], P('dp'), may hold values from 0.5 to 1.5
- cotangent: bfloat16 [6144, 2304], P(('dp', 'tensor')), may hold values from -6 to 6
Outputs:
- layer_output: bfloat16 [6144, 2304], P(('dp', 'tensor'))
- grad_tokens: float32 [6144, 2304], P(('dp', 'tensor'))
- grad_attention_norm: float32 [2304], P('dp')
- grad_query_weight: float32 [2304, 2048], P('dp', 'tensor')
- grad_key_weight: float32 [2304, 1024], P('dp', 'tensor')
- grad_value_weight: float32 [2304, 1024], P('dp', 'tensor')
- grad_output_weight: float32 [2048, 2304], P('tensor', 'dp')
- grad_attention_post_norm: float32 [2304], P('dp')
- grad_feedforward_norm: float32 [2304], P('dp')
- grad_gate_weight: float32 [2304, 9216], P('dp', 'tensor')
- grad_up_weight: float32 [2304, 9216], P('dp', 'tensor')
- grad_down_weight: float32 [9216, 2304], P('tensor', 'dp')
- grad_feedforward_post_norm: float32 [2304], P('dp')
The draws below stay inside these ranges and needn't reach their ends.
Inputs may be any that keep to these rules, and one draw needn't show every extreme that they name: `segment_ids`: within each aligned block of 768 rows (the tokens of one index of dp) the ids start at 0, never fall and rise by at most one from row to row; some block in every draw holds a single sequence of 768 tokens, and some block reaches the largest id.
All inputs are finite; a program needn't handle non-finite values.
Results may differ from the reference program's by a relative error of at most 0.024.
Values may be sent and summed in bfloat16 or wider, within the bound.
No kernel may reach another device: no remote copies, remote signals or barrier semaphores. Data moves between devices by JAX's collectives and lax.ppermute only.
A program may use at most 256 MiB of HBM per device.

```python
import math
import jax
import jax.numpy as jnp
from jax import lax

MODEL_WIDTH = 2304
QUERY_HEAD_COUNT = 8
KEY_VALUE_HEADS = 4
HEAD_WIDTH = 256
FF = 9216
TOK_DEV = 768
TOKENS = 6144


def draw_segment_ids(key, part):
    groups = TOKENS // TOK_DEV
    most_ids = max(TOK_DEV // 64, 2)
    stride = TOK_DEV // most_ids
    key_rate, key_cut, key_pick, key_whole = jax.random.split(key, 4)
    spacing = TOK_DEV // 2 ** jax.random.randint(key_rate, (groups, 1), 1, 4)
    cuts = jax.random.randint(key_cut, (groups, TOK_DEV), 0, spacing) == 0
    chosen = jax.random.randint(key_pick, (), 0, groups)
    busy_block = (chosen + 1) % groups
    block_index = jnp.arange(groups)[:, None]
    row_index = jnp.arange(TOK_DEV)[None, :]
    whole = (jax.random.randint(key_whole, (groups, 1), 0, 4) == 0) | (block_index == chosen)
    whole = whole & (block_index != busy_block)
    regular = row_index % stride == 0
    cuts = jnp.where(block_index == busy_block, regular, cuts)
    first = row_index == 0
    cuts = cuts & jnp.logical_not(whole) & jnp.logical_not(first)
    ids = jnp.cumsum(cuts.astype(jnp.int32), axis=1).astype(jnp.int32)
    ids = jnp.minimum(ids, most_ids - 1).astype(jnp.int32)
    return ids.reshape(TOKENS)


def level_of(own_key, extent, cuts, smallest, largest):
    def one(axis_at, parts):
        heights = jax.random.uniform(jax.random.fold_in(jax.random.fold_in(own_key, 6), axis_at), (parts,), jnp.float32, smallest / len(cuts), largest / len(cuts))
        return jnp.repeat(jnp.exp(heights), extent[axis_at] // parts).reshape((-1,) + (1,) * (len(extent) - axis_at - 1))

    factor_of = one(*cuts[0])
    for cut in cuts[1:]:
        factor_of = factor_of * one(*cut)
    return factor_of


def normal_values(key, extent, width, bound, cuts=(), kind=jnp.bfloat16):
    entries = width * jax.random.normal(key, extent, jnp.float32)
    if cuts:
        entries = entries * level_of(key, extent, cuts, -0.22, 0.18)
    return jnp.clip(entries, -bound, bound).astype(kind)


def setup_inputs(seed: int = 0) -> dict:
    arg_keys = jax.random.split(jax.random.key(seed), 15)
    return {
        "tokens": normal_values(arg_keys[0], (TOKENS, MODEL_WIDTH), 1.0, 6.0, ((0, 32),)),
        "segment_ids": draw_segment_ids(jax.random.fold_in(arg_keys[14], 71), 0),
        "attention_norm": jnp.clip(1.0 + 0.1 * jax.random.normal(arg_keys[2], (MODEL_WIDTH,), jnp.float32), 0.5, 1.5).astype(jnp.bfloat16),
        "query_weight": normal_values(arg_keys[3], (MODEL_WIDTH, QUERY_HEAD_COUNT * HEAD_WIDTH), MODEL_WIDTH ** -0.5, 0.125, ((0, 8), (1, 4))),
        "key_matrix": normal_values(arg_keys[4], (MODEL_WIDTH, KEY_VALUE_HEADS * HEAD_WIDTH), MODEL_WIDTH ** -0.5, 0.125, ((0, 8), (1, 4))),
        "value_matrix": normal_values(arg_keys[5], (MODEL_WIDTH, KEY_VALUE_HEADS * HEAD_WIDTH), MODEL_WIDTH ** -0.5, 0.125, ((0, 8), (1, 4))),
        "output_weight": normal_values(arg_keys[6], (QUERY_HEAD_COUNT * HEAD_WIDTH, MODEL_WIDTH), (QUERY_HEAD_COUNT * HEAD_WIDTH // 4) ** -0.5, 0.25, ((0, 4), (1, 8))),
        "attention_post_norm": jnp.clip(1.0 + 0.1 * jax.random.normal(arg_keys[7], (MODEL_WIDTH,), jnp.float32), 0.5, 1.5).astype(jnp.bfloat16),
        "feedforward_norm": jnp.clip(1.0 + 0.1 * jax.random.normal(arg_keys[8], (MODEL_WIDTH,), jnp.float32), 0.5, 1.5).astype(jnp.bfloat16),
        "gate_weight": normal_values(arg_keys[9], (MODEL_WIDTH, FF), MODEL_WIDTH ** -0.5, 0.125, ((0, 8), (1, 4))),
        "up_weight": normal_values(arg_keys[10], (MODEL_WIDTH, FF), MODEL_WIDTH ** -0.5, 0.125, ((0, 8), (1, 4))),
        "down_weight": normal_values(arg_keys[11], (FF, MODEL_WIDTH), FF ** -0.5, 0.0625, ((0, 4), (1, 8))),
        "feedforward_post_norm": jnp.clip(1.0 + 0.1 * jax.random.normal(arg_keys[12], (MODEL_WIDTH,), jnp.float32), 0.5, 1.5).astype(jnp.bfloat16),
        "cotangent": normal_values(arg_keys[13], (TOKENS, MODEL_WIDTH), 1.0, 6.0, ((0, 32),)),
    }


EPS = 1e-06
CAP = 50.0
HIGH = lax.Precision.HIGHEST

@jax.custom_vjp
def lowered_copy(v):
    return lax.optimization_barrier(v.astype(jnp.bfloat16)).astype(jnp.float32)

@jax.custom_vjp
def lowered_pullback(v):
    return v

def low_keep(v):
    return (lowered_copy(v), None)

def low_pass(kept, grad):
    return (grad,)

def back_keep(v):
    return (v, None)

def back_low(kept, grad):
    return (lowered_copy(grad),)
lowered_copy.defvjp(low_keep, low_pass)
lowered_pullback.defvjp(back_keep, back_low)

def matrix_product(left, right):
    return jnp.dot(left, right, precision=HIGH, preferred_element_type=jnp.float32)

def rms_norm(values, gains):
    return values * lax.rsqrt(lax.optimization_barrier(jnp.mean(values * values, axis=-1, keepdims=True)) + EPS) * gains

def position_tables(segment_ids, head_size):
    row_count = segment_ids.shape[0]
    earlier = lax.optimization_barrier(jnp.sum((segment_ids[None, :] < segment_ids[:, None]).astype(jnp.int32), axis=1))
    place = (jnp.arange(row_count, dtype=jnp.int32) - earlier).astype(jnp.float32)
    half_size = head_size // 2
    freqs = jnp.exp(jnp.arange(half_size, dtype=jnp.float32) * (-2.0 * math.log(10000.0) / head_size))
    angles = place[:, None] * jnp.concatenate([freqs, freqs])[None, :]
    row_index = jnp.arange(row_count, dtype=jnp.int32)
    allowed = (segment_ids[None, :] == segment_ids[:, None]) & (row_index[None, :] <= row_index[:, None])
    return (jnp.cos(angles)[:, None, :], jnp.sin(angles)[:, None, :], allowed)

def rotary_apply(tensor, cosine_table, sine_table):
    half_size = tensor.shape[-1] // 2
    turned = jnp.concatenate([-tensor[..., half_size:], tensor[..., :half_size]], axis=-1)
    return tensor * cosine_table + turned * sine_table

def layer(inputs, gain_one, query_full, key_rows_full, value_rows_full, output_full, gain_two, gain_three, gate_full, up_full, down_full, gain_four, cosine_table, sine_table, allowed):
    token_rows = inputs.shape[0]
    group_width = QUERY_HEAD_COUNT // KEY_VALUE_HEADS
    attention_input = lowered_copy(rms_norm(inputs, gain_one))
    query_unrotated = lowered_pullback(matrix_product(attention_input, query_full)).reshape(token_rows, QUERY_HEAD_COUNT, HEAD_WIDTH)
    key_unrotated = lowered_pullback(matrix_product(attention_input, key_rows_full)).reshape(token_rows, KEY_VALUE_HEADS, HEAD_WIDTH)
    value_projected = lowered_pullback(matrix_product(attention_input, value_rows_full)).reshape(token_rows, KEY_VALUE_HEADS, HEAD_WIDTH)
    query_rows = lowered_copy(rotary_apply(query_unrotated, cosine_table, sine_table) * HEAD_WIDTH ** (-0.5)).reshape(token_rows, KEY_VALUE_HEADS, group_width, HEAD_WIDTH)
    keys = lowered_copy(rotary_apply(key_unrotated, cosine_table, sine_table))
    values = lowered_copy(value_projected)
    scores = lowered_pullback(jnp.einsum('qkgd,skd->kgqs', query_rows, keys, precision=HIGH))
    capped = CAP * jnp.tanh(scores / CAP)
    expo = jnp.where(allowed[None, None], jnp.exp(capped), 0.0)
    probs = lowered_copy(expo / lax.optimization_barrier(jnp.sum(expo, axis=-1, keepdims=True)))
    mixed = jnp.einsum('kgqs,skd->qkgd', probs, values, precision=HIGH).reshape(token_rows, QUERY_HEAD_COUNT * HEAD_WIDTH)
    mixed = lowered_copy(lowered_pullback(mixed))
    attn_branch = lowered_pullback(matrix_product(mixed, output_full))
    middle = inputs + rms_norm(attn_branch, gain_two)
    ffn_in = lowered_copy(rms_norm(middle, gain_three))
    gate = lowered_pullback(matrix_product(ffn_in, gate_full))
    up_values = lowered_pullback(matrix_product(ffn_in, up_full))
    hidden = lowered_copy(jax.nn.gelu(gate, approximate=True) * up_values)
    ffn_branch = lowered_pullback(matrix_product(hidden, down_full))
    return middle + rms_norm(ffn_branch, gain_four)

def reference(tokens, segment_ids, attention_norm, query_weight, key_matrix, value_matrix, output_weight, attention_post_norm, feedforward_norm, gate_weight, up_weight, down_weight, feedforward_post_norm, cotangent):
    groups = TOKENS // TOK_DEV
    params = tuple((item.astype(jnp.float32) for item in (attention_norm, query_weight, key_matrix, value_matrix, output_weight, attention_post_norm, feedforward_norm, gate_weight, up_weight, down_weight, feedforward_post_norm)))
    inputs_all = tokens.astype(jnp.float32).reshape(groups, TOK_DEV, MODEL_WIDTH)
    cot_all = cotangent.astype(jnp.float32).reshape(groups, TOK_DEV, MODEL_WIDTH)
    segs_all = segment_ids.reshape(groups, TOK_DEV)

    def one_block(totals, items):
        inputs, segments, cot_block = items
        cosine_table, sine_table, allowed = position_tables(segments, HEAD_WIDTH)

        def forward(inputs_in, *weights):
            return layer(inputs_in, *weights, cosine_table, sine_table, allowed)
        result, pullback = jax.vjp(forward, inputs, *params)
        grads = pullback(cot_block)
        totals = tuple((total + grad for total, grad in zip(totals, grads[1:])))
        return (totals, (result, grads[0]))
    starting = tuple((jnp.zeros_like(item) for item in params))
    totals, (results, grad_inputs) = lax.scan(one_block, starting, (inputs_all, segs_all, cot_all))
    layer_output = results.reshape(TOKENS, MODEL_WIDTH).astype(jnp.bfloat16)
    grad_tokens = grad_inputs.reshape(TOKENS, MODEL_WIDTH)
    return (layer_output, grad_tokens, totals[0], totals[1], totals[2], totals[3], totals[4], totals[5], totals[6], totals[7], totals[8], totals[9], totals[10])
```

```python
import math

import jax
import jax.numpy as jnp
from jax import lax
from jax.sharding import PartitionSpec as P

HEAD_WIDTH = 256
EPS = 1e-06
CAP = 50.0
BF16 = jnp.bfloat16
F32 = jnp.float32


def rms_norm(values, gains):
    return values * lax.rsqrt(jnp.mean(values * values, axis=-1, keepdims=True) + EPS) * gains


def norm_back(values, gains, grads):
    ignored, pullback = jax.vjp(rms_norm, values, gains)
    return pullback(grads)


def position_tables(segment_ids, head_size):
    row_count = segment_ids.shape[0]
    earlier = jnp.sum((segment_ids[None, :] < segment_ids[:, None]).astype(jnp.int32), axis=1)
    place = (jnp.arange(row_count, dtype=jnp.int32) - earlier).astype(F32)
    half_size = head_size // 2
    freqs = jnp.exp(jnp.arange(half_size, dtype=F32) * (-2.0 * math.log(10000.0) / head_size))
    angles = place[:, None] * jnp.concatenate([freqs, freqs])[None, :]
    row_index = jnp.arange(row_count, dtype=jnp.int32)
    allowed = (segment_ids[None, :] == segment_ids[:, None]) & (
        row_index[None, :] <= row_index[:, None]
    )
    return (jnp.cos(angles)[:, None, :], jnp.sin(angles)[:, None, :], allowed)


def rotary_apply(tensor, cosine_table, sine_table):
    half_size = tensor.shape[-1] // 2
    turned = jnp.concatenate([-tensor[..., half_size:], tensor[..., :half_size]], axis=-1)
    return tensor * cosine_table + turned * sine_table


def rotate_back(tensor, cosine_table, sine_table):
    half_size = tensor.shape[-1] // 2
    weighted = tensor * sine_table
    turned = jnp.concatenate([weighted[..., half_size:], -weighted[..., :half_size]], axis=-1)
    return tensor * cosine_table + turned


def contract_rows(left, right):
    return lax.dot_general(left, right, (((0,), (0,)), ((), ())), preferred_element_type=F32)


def contract_cols(left, right):
    return lax.dot_general(left, right, (((1,), (1,)), ((), ())), preferred_element_type=F32)


def matmul(left, right):
    return jnp.dot(left, right, preferred_element_type=F32)


def attend(query_rows, keys, values, allowed):
    scores = jnp.einsum("qkgd,skd->kgqs", query_rows, keys, preferred_element_type=F32)
    capped = CAP * jnp.tanh(scores / CAP)
    expo = jnp.where(allowed[None, None], jnp.exp(capped), 0.0)
    totals = jnp.sum(expo, axis=-1, keepdims=True)
    probs = (expo / totals).astype(BF16)
    mixed = jnp.einsum("kgqs,skd->qkgd", probs, values, preferred_element_type=F32)
    return (mixed, jnp.log(totals))


def attend_back(query_rows, keys, values, allowed, log_total, grad_mixed):
    scores = jnp.einsum("qkgd,skd->kgqs", query_rows, keys, preferred_element_type=F32)
    ratio = jnp.tanh(scores / CAP)
    probs = jnp.where(allowed[None, None], jnp.exp(CAP * ratio - log_total), 0.0)
    grad_values = jnp.einsum(
        "kgqs,qkgd->skd", probs.astype(BF16), grad_mixed, preferred_element_type=F32
    )
    grad_probs = jnp.einsum("qkgd,skd->kgqs", grad_mixed, values, preferred_element_type=F32)
    grad_capped = probs * (grad_probs - jnp.sum(probs * grad_probs, axis=-1, keepdims=True))
    grad_scores = (grad_capped * (1.0 - ratio * ratio)).astype(BF16)
    grad_queries = jnp.einsum("kgqs,skd->qkgd", grad_scores, keys, preferred_element_type=F32)
    grad_keys = jnp.einsum("kgqs,qkgd->skd", grad_scores, query_rows, preferred_element_type=F32)
    return (grad_queries, grad_keys, grad_values)


class Swaps:
    def __init__(self, dp_count, tensor_count):
        self.dp_count = dp_count
        self.tensor_count = tensor_count
        self.dp = lax.axis_index("dp")
        self.tensor = lax.axis_index("tensor")
        bits = [1 << k for k in range(dp_count.bit_length() - 1)]
        self.split = 2
        self.far = [b for b in reversed(bits) if b != 2 and b != 1]
        self.near = 1
        self.all_bits = list(reversed(bits))
        self.tensor_bits = [1 << k for k in range(tensor_count.bit_length() - 1)]

    def over_dp(self, value, bit):
        return lax.ppermute(value, "dp", [(i, i ^ bit) for i in range(self.dp_count)])

    def over_tensor(self, value, bit):
        return lax.ppermute(value, "tensor", [(i, i ^ bit) for i in range(self.tensor_count)])

    def on_dp(self, bit):
        return (self.dp & bit) != 0

    def on_tensor(self, bit):
        return (self.tensor & bit) != 0


def gather_blocks(block, bits, swap):
    blocks = {0: block}
    for bit in bits:
        blocks.update({r | bit: swap(v, bit) for r, v in blocks.items()})
    return blocks


def place_blocks(blocks, me):
    count = len(blocks)
    rows = blocks[0].shape[0]
    out = jnp.zeros((count,) + blocks[0].shape, blocks[0].dtype)
    for r, v in blocks.items():
        out = lax.dynamic_update_slice_in_dim(out, v[None], me ^ r, 0)
    return out.reshape((count * rows,) + blocks[0].shape[1:])


def pick(blocks, index):
    return lax.dynamic_index_in_dim(blocks, index, 0, keepdims=False)


def add_low(left, right):
    return (left.astype(F32) + right.astype(F32)).astype(BF16)


def sum_blocks(full, bits, me, swap):
    count = 1 << len(bits)
    blocks = full.reshape((count, full.shape[0] // count) + full.shape[1:])
    held = {r: pick(blocks, me ^ r) for r in range(count)}
    for step, bit in enumerate(bits):
        last = step == len(bits) - 1
        for r in [r for r in sorted(held, reverse=True) if r & bit]:
            got = swap(held.pop(r), bit)
            keep = r ^ bit
            if last:
                held[keep] = held[keep].astype(F32) + got.astype(F32)
            else:
                held[keep] = add_low(held[keep], got)
    return held[0]


def body(dp_count, tensor_count, *args):
    (
        tokens,
        segment_ids,
        attention_norm,
        query_weight,
        key_matrix,
        value_matrix,
        output_weight,
        attention_post_norm,
        feedforward_norm,
        gate_weight,
        up_weight,
        down_weight,
        feedforward_post_norm,
        cotangent,
    ) = args
    net = Swaps(dp_count, tensor_count)
    core_bit, chip_bit = 1, 2
    rows = tokens.shape[0]
    query_width = query_weight.shape[1]
    key_width = key_matrix.shape[1]
    query_heads = query_width // HEAD_WIDTH
    key_heads = key_width // HEAD_WIDTH
    group_width = query_heads // key_heads
    query_scale = HEAD_WIDTH ** (-0.5)

    gains = jnp.stack([attention_norm, attention_post_norm, feedforward_norm, feedforward_post_norm])
    every_gain = place_blocks(gather_blocks(gains[None], net.all_bits, net.over_dp), net.dp)
    every_gain = every_gain.transpose(1, 0, 2).reshape(4, -1).astype(F32)
    gain_one, gain_two, gain_three, gain_four = (every_gain[k] for k in range(4))

    qkv_own = jnp.concatenate([query_weight, key_matrix, value_matrix], axis=1)
    out_own = output_weight.T
    qkv_blocks = gather_blocks(qkv_own, net.all_bits, net.over_dp)
    out_blocks = gather_blocks(out_own, net.all_bits, net.over_dp)
    qkv_full = place_blocks(qkv_blocks, net.dp)
    out_full = place_blocks(out_blocks, net.dp)

    def ffn_gather(weight):
        half = weight.shape[1] // 2
        low, high = weight[:, :half], weight[:, half:]
        upper = net.on_dp(net.split)
        keep = jnp.where(upper, high, low)
        send = jnp.where(upper, low, high)
        blocks = {0: keep, net.split: net.over_dp(send, net.split)}
        for bit in net.far + [net.near]:
            blocks.update({r | bit: net.over_dp(v, bit) for r, v in blocks.items()})
        return place_blocks(blocks, net.dp)

    gate_full = ffn_gather(gate_weight)
    up_full = ffn_gather(up_weight)
    down_full = ffn_gather(down_weight.T)

    def block_gather(own):
        blocks = gather_blocks(own, [chip_bit, core_bit], net.over_tensor)
        return place_blocks(blocks, net.tensor)

    def block_sum(full):
        return sum_blocks(full, [core_bit, chip_bit], net.tensor, net.over_tensor)

    half_rows = rows // 2

    def wide_gather(own):
        from_y = net.over_tensor(own, chip_bit)
        from_z = net.over_dp(own, net.split)
        far_low = net.over_dp(from_y[:half_rows], net.split)
        far_high = net.over_tensor(from_z[half_rows:], chip_bit)
        pieces = [own, from_y, from_z, far_low, far_high]
        others = [net.over_tensor(p, core_bit) for p in pieces]
        return jnp.concatenate(pieces + others, axis=0)

    def wide_sum(full):
        mine, theirs = full[: 4 * rows], full[4 * rows :]
        part = mine.astype(F32) + net.over_tensor(theirs.astype(BF16), core_bit).astype(F32)
        own, to_y, to_z, far = (part[k * rows : (k + 1) * rows] for k in range(4))
        far = far.astype(BF16)
        got_low = net.over_dp(far[:half_rows], net.split)
        got_high = net.over_tensor(far[half_rows:], chip_bit)
        to_y = jnp.concatenate([to_y[:half_rows] + got_low.astype(F32), to_y[half_rows:]], axis=0)
        to_z = jnp.concatenate([to_z[:half_rows], to_z[half_rows:] + got_high.astype(F32)], axis=0)
        own = own + net.over_tensor(to_y.astype(BF16), chip_bit).astype(F32)
        return own + net.over_dp(to_z.astype(BF16), net.split).astype(F32)

    cosine_table, sine_table, allowed = position_tables(segment_ids, HEAD_WIDTH)
    inputs = tokens.astype(F32)
    attention_input = rms_norm(inputs, gain_one).astype(BF16)
    attn_rows = block_gather(attention_input)
    group_rows = attn_rows.shape[0]
    projected = matmul(attn_rows, qkv_full)
    query_unrotated = projected[:, :query_width].reshape(group_rows, query_heads, HEAD_WIDTH)
    key_unrotated = projected[:, query_width : query_width + key_width].reshape(
        group_rows, key_heads, HEAD_WIDTH
    )
    query_rows = (
        (rotary_apply(query_unrotated, cosine_table, sine_table) * query_scale)
        .astype(BF16)
        .reshape(group_rows, key_heads, group_width, HEAD_WIDTH)
    )
    keys = rotary_apply(key_unrotated, cosine_table, sine_table).astype(BF16)
    values = (
        projected[:, query_width + key_width :]
        .astype(BF16)
        .reshape(group_rows, key_heads, HEAD_WIDTH)
    )
    mixed_wide, log_total = attend(query_rows, keys, values, allowed)
    mixed = mixed_wide.reshape(group_rows, query_width).astype(BF16)
    attn_branch = block_sum(contract_cols(mixed, out_full).astype(BF16))
    middle = inputs + rms_norm(attn_branch, gain_two)

    ffn_in = rms_norm(middle, gain_three).astype(BF16)
    ffn_rows = wide_gather(ffn_in)
    gate_values = matmul(ffn_rows, gate_full)
    up_values = matmul(ffn_rows, up_full)
    hidden = (jax.nn.gelu(gate_values, approximate=True) * up_values).astype(BF16)
    ffn_branch = wide_sum(contract_cols(hidden, down_full))
    layer_output = (middle + rms_norm(ffn_branch, gain_four)).astype(BF16)

    grad_out = cotangent.astype(F32)
    grad_ffn_branch, grad_gain_four = norm_back(ffn_branch, gain_four, grad_out)
    grad_ffn_rows = wide_gather(grad_ffn_branch.astype(BF16))
    grad_down_full = contract_rows(grad_ffn_rows, hidden).astype(BF16)
    grad_hidden = matmul(grad_ffn_rows, down_full)
    ignored, gelu_pull = jax.vjp(
        lambda gate_in, up_in: jax.nn.gelu(gate_in, approximate=True) * up_in,
        gate_values,
        up_values,
    )
    grad_gate_wide, grad_up_wide = gelu_pull(grad_hidden)
    grad_gate_low = grad_gate_wide.astype(BF16)
    grad_up_low = grad_up_wide.astype(BF16)
    grad_gate_full = contract_rows(ffn_rows, grad_gate_low).astype(BF16)
    grad_up_full = contract_rows(ffn_rows, grad_up_low).astype(BF16)
    grad_ffn_in = wide_sum(
        contract_cols(grad_gate_low, gate_full) + contract_cols(grad_up_low, up_full)
    )

    def ffn_reduce(full):
        width = full.shape[1]
        blocks = full.reshape(dp_count, full.shape[0] // dp_count, width)
        held = {r: pick(blocks, net.dp ^ r) for r in range(dp_count)}
        bits = [net.near] + net.far
        for step, bit in enumerate(bits):
            last = step == len(bits) - 1
            for r in [r for r in sorted(held, reverse=True) if r & bit]:
                got = net.over_dp(held.pop(r), bit)
                keep = r ^ bit
                if last and keep == 0:
                    held[keep] = held[keep].astype(F32) + got.astype(F32)
                else:
                    held[keep] = add_low(held[keep], got)
        other = net.over_dp(held[net.split], net.split).astype(F32)
        upper = net.on_dp(net.split)
        return jnp.concatenate(
            [jnp.where(upper, other, held[0]), jnp.where(upper, held[0], other)], axis=1
        )

    grad_down = ffn_reduce(grad_down_full).T
    grad_gate = ffn_reduce(grad_gate_full)
    grad_up = ffn_reduce(grad_up_full)

    grad_middle_part, grad_gain_three = norm_back(middle, gain_three, grad_ffn_in)
    grad_middle = grad_out + grad_middle_part

    grad_attn_branch, grad_gain_two = norm_back(attn_branch, gain_two, grad_middle)
    grad_attn_rows = block_gather(grad_attn_branch.astype(BF16))
    grad_output_full = contract_rows(grad_attn_rows, mixed).astype(BF16)
    grad_mixed = (
        matmul(grad_attn_rows, out_full)
        .astype(BF16)
        .reshape(group_rows, key_heads, group_width, HEAD_WIDTH)
    )
    grad_queries, grad_keys, grad_values = attend_back(
        query_rows, keys, values, allowed, log_total, grad_mixed
    )
    grad_query_low = (
        rotate_back(
            grad_queries.reshape(group_rows, query_heads, HEAD_WIDTH) * query_scale,
            cosine_table,
            sine_table,
        )
        .reshape(group_rows, query_width)
        .astype(BF16)
    )
    grad_key_low = (
        rotate_back(grad_keys, cosine_table, sine_table).reshape(group_rows, key_width).astype(BF16)
    )
    grad_value_low = grad_values.reshape(group_rows, key_width).astype(BF16)
    grad_projected = jnp.concatenate([grad_query_low, grad_key_low, grad_value_low], axis=1)
    grad_qkv_full = contract_rows(attn_rows, grad_projected).astype(BF16)
    grad_attn_in = block_sum(contract_cols(grad_projected, qkv_full).astype(BF16))
    grad_input_part, grad_gain_one = norm_back(inputs, gain_one, grad_attn_in)
    grad_tokens = grad_middle + grad_input_part

    dp_bits = list(reversed(net.all_bits))
    grad_out_own = sum_blocks(grad_output_full, dp_bits, net.dp, net.over_dp).T
    grad_qkv_own = sum_blocks(grad_qkv_full, dp_bits, net.dp, net.over_dp)

    grad_gains = jnp.stack([grad_gain_one, grad_gain_two, grad_gain_three, grad_gain_four])
    for bit in net.tensor_bits:
        grad_gains = grad_gains + net.over_tensor(grad_gains, bit)
    gain_parts = grad_gains.reshape(4, dp_count, -1).transpose(1, 0, 2)
    for bit in net.all_bits:
        count = gain_parts.shape[0] // 2
        upper = net.on_dp(bit)
        keep = jnp.where(upper, gain_parts[count:], gain_parts[:count])
        send = jnp.where(upper, gain_parts[:count], gain_parts[count:])
        gain_parts = keep + net.over_dp(send, bit)
    gain_sums = gain_parts[0]
    return (
        layer_output,
        grad_tokens,
        gain_sums[0],
        grad_qkv_own[:, :query_width],
        grad_qkv_own[:, query_width : query_width + key_width],
        grad_qkv_own[:, query_width + key_width :],
        grad_out_own,
        gain_sums[1],
        gain_sums[2],
        grad_gate,
        grad_up,
        grad_down,
        gain_sums[3],
    )


def solution(mesh):
    row = P(("dp", "tensor"), None)
    columns = P("dp", "tensor")
    turned = P("tensor", "dp")
    gain = P("dp")
    in_specs = (
        row,
        gain,
        gain,
        columns,
        columns,
        columns,
        turned,
        gain,
        gain,
        columns,
        columns,
        turned,
        gain,
        row,
    )
    out_specs = (
        row,
        row,
        gain,
        columns,
        columns,
        columns,
        turned,
        gain,
        gain,
        columns,
        columns,
        turned,
        gain,
    )
    dp_count, tensor_count = mesh.shape["dp"], mesh.shape["tensor"]

    def run(*args):
        return body(dp_count, tensor_count, *args)

    return jax.shard_map(run, mesh=mesh, in_specs=in_specs, out_specs=out_specs, check_vma=False)
```
